32 devices in a mesh: row: 16 (over z, y, x), col: 2 (over core).
Axes of the slice: x: 2, y: 2, z: 4, core: 2. Of those that a mesh axis runs over, the one named last changes fastest.
Arguments:
- features: bfloat16 [16384, 1024], P(('row', 'col')), may hold values from -5 to 5
- sketch: bfloat16 [16384, 640], P(('row', 'col')), may hold values from -6 to 6
- near_blocks: int32 [16, 4], P('row'), may hold values from 0 to 15, as said below
Outputs:
- leaf_basis: float32 [16384, 512], P(('row', 'col'))
- oversample_residual: float32 [16384, 128], P(('row', 'col'))
- node_factors: float32 [16, 4, 512, 512], P('row', None, 'col')
The draws below stay inside these ranges and needn't reach their ends.
Inputs may be any that keep to these rules, and one draw needn't show every extreme that they name: `near_blocks`: row b starts with b itself, followed by 4 - 1 distinct other blocks at distance 1 to 3 from b.
All inputs are finite; a program needn't handle non-finite values.
Results may differ from the reference program's by a relative error of at most 0.004.
Values may be sent and summed in bfloat16 or wider, within the bound.
A program may use at most 64 MiB of HBM per device.

```python
import math
import jax
import jax.numpy as jnp
from jax import lax

D = 1024
LEAF = 1024
RANK = 512
OVER = 128
NEAR = 4
NEIGHBOR = 3
LEVELS = 3
SKETCH = 640
NBLK = 16
ROWS = 16384


def draw_features(key, part):
    basis_count = max(D // 16, 8)
    directions = jax.random.normal(jax.random.fold_in(key, 3), (basis_count, D), jnp.float32)
    private = jax.random.normal(jax.random.fold_in(key, 1), (ROWS, D), jnp.float32)
    loadings = jax.random.normal(jax.random.fold_in(key, 2), (ROWS, basis_count), jnp.float32)
    shared = jnp.dot(loadings, directions, precision=lax.Precision.HIGHEST) * (1.0 / math.sqrt(basis_count))
    values = 0.63 * private + 1.26 * shared
    values = jnp.clip(values, -5.0, 5.0)
    return values.astype(jnp.bfloat16)


def draw_near_blocks(key, part):
    spread = NEIGHBOR
    offsets = jnp.concatenate([jnp.arange(-spread, 0, dtype=jnp.int32), jnp.arange(1, spread + 1, dtype=jnp.int32)])
    blocks = jnp.arange(NBLK, dtype=jnp.int32)[:, None]
    targets = blocks + offsets[None, :]
    inside = (targets >= 0) & (targets < NBLK)
    scores = jax.random.randint(jax.random.fold_in(key, 11), (NBLK, 2 * spread), 0, 1000, dtype=jnp.int32) * (2 * spread) + jnp.arange(2 * spread, dtype=jnp.int32)[None, :]
    scores = jnp.where(inside, scores, -1)
    best_scores, picks = lax.top_k(scores, NEAR - 1)
    chosen = jnp.take_along_axis(targets, picks, axis=1)
    return jnp.concatenate([blocks, chosen], axis=1).astype(jnp.int32)


def levels(key, dims, pieces, low, largest):
    def one(axis_at, parts):
        draws = jax.random.uniform(jax.random.fold_in(jax.random.fold_in(key, 6), axis_at), (parts,), jnp.float32, low / len(pieces), largest / len(pieces))
        return jnp.repeat(jnp.exp(draws), dims[axis_at] // parts).reshape((-1,) + (1,) * (len(dims) - axis_at - 1))

    factor_of = one(*pieces[0])
    for cut in pieces[1:]:
        factor_of = factor_of * one(*cut)
    return factor_of


def scatter_about(stream_key, extent, deviation, most, cuts=(), kind=jnp.bfloat16):
    values = deviation * jax.random.normal(stream_key, extent, jnp.float32)
    if cuts:
        values = values * levels(stream_key, extent, cuts, -0.22, 0.18)
    return jnp.clip(values, -most, most).astype(kind)


def setup_inputs(seed: int = 0) -> dict:
    seeds = jax.random.split(jax.random.key(seed), 4)
    features = draw_features(jax.random.fold_in(seeds[3], 71), 0)
    sketch = scatter_about(seeds[1], (ROWS, SKETCH), 1.0, 6.0, ((0, 32),))
    near_blocks = draw_near_blocks(jax.random.fold_in(seeds[3], 71), 0)
    return dict(features=features, sketch=sketch, near_blocks=near_blocks)


highest = lax.Precision.HIGHEST

def sample_block(features, sketch, near_blocks, block_index):
    inv_width = 1.0 / D
    sample_norm = 1.0 / math.sqrt(8 * NEAR * LEAF)
    first_row = (block_index * LEAF).astype(jnp.int32)
    own_rows = lax.dynamic_slice_in_dim(features, first_row, LEAF, 0)
    own_sketch = lax.dynamic_slice_in_dim(sketch, first_row, LEAF, 0).astype(jnp.float32)
    running = jnp.zeros((LEAF, RANK + OVER), jnp.float32)
    for entry_index in range(NEAR):
        other_block = near_blocks[block_index, entry_index].astype(jnp.int32)
        other_first = (other_block * LEAF).astype(jnp.int32)
        other_rows = lax.dynamic_slice_in_dim(features, other_first, LEAF, 0)
        other_sketch = lax.dynamic_slice_in_dim(sketch, other_first, LEAF, 0)
        scores = lax.dot_general(own_rows.astype(jnp.float32), other_rows.astype(jnp.float32), (((1,), (1,)), ((), ())), preferred_element_type=jnp.float32) * inv_width
        kernel = jnp.exp(scores).astype(jnp.bfloat16)
        running = running + jnp.dot(kernel.astype(jnp.float32), other_sketch.astype(jnp.float32), preferred_element_type=jnp.float32)
    sample = running * sample_norm + 0.5 * own_sketch
    gram_matrix = lax.dot_general(sample.astype(jnp.float32), sample.astype(jnp.float32), (((0,), (0,)), ((), ())), precision=highest, preferred_element_type=jnp.float32) / LEAF
    return (sample, gram_matrix)

def reference(features, sketch, near_blocks):
    block_ids = jnp.arange(NBLK, dtype=jnp.int32)
    samples, grams = lax.map(lambda block_index: sample_block(features, sketch, near_blocks, block_index), block_ids)
    level_gram = grams[:, :RANK, :RANK]
    lowers = [jnp.linalg.cholesky(level_gram)]
    for depth_level in range(LEVELS):
        partner = jnp.bitwise_xor(block_ids, jnp.int32(1 << depth_level))
        level_gram = (level_gram + level_gram[partner]) * 0.5
        lowers.append(jnp.linalg.cholesky(level_gram))
    node_factors = jnp.swapaxes(jnp.stack(lowers, axis=1), 2, 3)
    lower_leaf = lowers[0]
    leaf_basis = lax.linalg.triangular_solve(lower_leaf, samples[:, :, :RANK], left_side=False, lower=True, transpose_a=True)
    coupling = lax.linalg.triangular_solve(lower_leaf, grams[:, :RANK, RANK:], left_side=True, lower=True)
    residual = samples[:, :, RANK:] - jnp.einsum('blr,bro->blo', leaf_basis, coupling, precision=highest)
    return (leaf_basis.reshape(ROWS, RANK), residual.reshape(ROWS, OVER), node_factors)
```

```python
import functools
import math

import jax
import jax.numpy as jnp
from jax import lax
from jax.experimental import pallas as pl
from jax.experimental.pallas import tpu as pltpu
from jax.sharding import PartitionSpec as P

D = 1024
LEAF = 1024
RANK = 512
NEAR = 4
NEIGHBOR = 3
LEVELS = 3
T = 128
NB = 32
F32 = jnp.float32

def split(x):
    hi = x.astype(jnp.bfloat16)
    return hi, (x - hi.astype(F32)).astype(jnp.bfloat16)

def mm(a, b, dims=(((1,), (0,)), ((), ()))):
    ah, al = split(a); bh, bl = split(b)
    d = functools.partial(lax.dot_general, dimension_numbers=dims, preferred_element_type=F32)
    return d(ah, bh) + (d(ah, bl) + d(al, bh))

TN = (((0,), (0,)), ((), ()))
NT = (((1,), (1,)), ((), ()))

def factor_kernel(slab, gram_ref, level_ref, sample_ref, first_ref, leaf_ref, resid_ref, fac_ref, work, d, panel, y):
    rank = level_ref.shape[1]
    over = sample_ref.shape[1] - rank
    count = 1 + level_ref.shape[0]
    tiles = rank // T
    work[0] = gram_ref[...]
    for m in range(1, count):
        work[m, :, 0:rank] = level_ref[m - 1]
    y[...] = sample_ref[:, 0:rank]
    row_i = lax.broadcasted_iota(jnp.int32, (T, T), 0)
    col_i = lax.broadcasted_iota(jnp.int32, (T, T), 1)
    sub_row = lax.broadcasted_iota(jnp.int32, (NB, T), 0)
    lane = lax.broadcasted_iota(jnp.int32, (NB, T), 1)
    upper = row_i <= col_i
    for p in range(tiles):
        lo = p * T
        for m in range(count):
            d[m, :, 0:T] = work[m, lo:lo + T, lo:lo + T]
            d[m, :, T:2 * T] = jnp.where(row_i == col_i, 1.0, 0.0).astype(F32)

        def sub(s, carry):
            at = pl.multiple_of(s * NB, NB)
            shift = lax.rem(T - at, T)
            a = [pltpu.roll(d[m, pl.ds(at, NB), 0:T], shift, 1) for m in range(count)]
            e = [d[m, pl.ds(at, NB), T:2 * T] for m in range(count)]
            ua = [jnp.zeros((NB, T), F32) for _ in range(count)]
            scale = [jnp.zeros((NB, T), F32) for _ in range(count)]
            for j in range(NB):
                for m in range(count):
                    b = jnp.broadcast_to(a[m][:, j:j + 1], (NB, T))
                    rs = lax.rsqrt(jnp.broadcast_to(b[j:j + 1, :], (NB, T)))
                    pick = sub_row == j
                    scale[m] = jnp.where(pick, rs, scale[m])
                    if j < NB - 1:
                        f = jnp.where(sub_row > j, b * rs, 0.0)
                        a[m] = a[m] - f * (jnp.broadcast_to(a[m][j:j + 1, :], (NB, T)) * rs)
                        e[m] = e[m] - f * (jnp.broadcast_to(e[m][j:j + 1, :], (NB, T)) * rs)
            for m in range(count):
                u = pltpu.roll(a[m] * scale[m], at, 1)
                v = e[m] * scale[m]
                d[m, pl.ds(at, NB), 0:T] = u
                d[m, pl.ds(at, NB), T:2 * T] = v
                left = jnp.where(lane >= at + NB, u, 0.0)
                both = jnp.concatenate([u, v], axis=1)
                d[m] = d[m] - mm(left, both, TN)
            return carry

        lax.fori_loop(0, T // NB, sub, 0)
        for m in range(count):
            inv = d[m, :, T:2 * T]
            work[m, lo:lo + T, lo:lo + T] = jnp.where(upper, d[m, :, 0:T], 0.0)
            if p:
                work[m, lo:lo + T, 0:lo] = jnp.zeros((T, lo), F32)
            end = rank + (over if m == 0 else 0)
            if lo + T < end:
                u = mm(inv, work[m, lo:lo + T, lo + T:end])
                work[m, lo:lo + T, lo + T:end] = u
                for j in range(p + 1, tiles):
                    left = u[:, (j - p - 1) * T:(j - p) * T]
                    work[m, j * T:(j + 1) * T, j * T:end] = work[m, j * T:(j + 1) * T, j * T:end] - mm(left, u[:, (j - p - 1) * T:], TN)
            if m == 0:
                q = mm(y[:, lo:lo + T], inv, NT)
                leaf_ref[:, lo:lo + T] = q
                if p + 1 < tiles:
                    y[:, lo + T:rank] = y[:, lo + T:rank] - mm(q, u[:, 0:rank - lo - T])
    resid_ref[...] = sample_ref[:, rank:] - mm(leaf_ref[...], work[0, :, rank:])
    first = pl.multiple_of(first_ref[0], slab)
    for m in range(count):
        fac_ref[m] = work[m, pl.ds(first, slab), 0:rank]

def factor(gram, level, sample, first, slab):
    rows, width = sample.shape
    rank = level.shape[1]
    count = 1 + level.shape[0]
    vm = pl.BlockSpec(memory_space=pltpu.VMEM)
    return pl.pallas_call(
        functools.partial(factor_kernel, slab),
        out_shape=(jax.ShapeDtypeStruct((rows, rank), F32),
                   jax.ShapeDtypeStruct((rows, width - rank), F32),
                   jax.ShapeDtypeStruct((count, slab, rank), F32)),
        in_specs=[vm, vm, vm, pl.BlockSpec(memory_space=pltpu.SMEM)],
        out_specs=(vm, vm, vm),
        scratch_shapes=[pltpu.VMEM((count, rank, width), F32), pltpu.VMEM((count, T, 2 * T), F32),
                        pltpu.VMEM((8, 128), F32), pltpu.VMEM((rows, rank), F32)],
        compiler_params=pltpu.CompilerParams(vmem_limit_bytes=48 * 2**20),
        name="factor",
    )(gram, level, sample, first)


GROUP = 4
CHUNKS = 4


def gather_kernel(peers, own, out, recv, send):
    row = lax.axis_index("row")
    col = lax.axis_index("col")
    q = lax.rem(row, GROUP)
    sx = 1 - 2 * lax.rem(q, 2)
    sy = 1 - 2 * (q // 2)
    middle = (q == 1) | (q == 2)
    outer = (q == 0) | (q == 3)
    rows = own.shape[0] // CHUNKS

    def exists(way):
        return (row + GROUP * way >= 0) & (row + GROUP * way < peers)

    def piece(c):
        return pl.ds(c * rows, rows)

    def copy(source, to_slot, c, kind, step):
        return pltpu.make_async_remote_copy(
            src_ref=source,
            dst_ref=out.at[to_slot, piece(c)],
            send_sem=send.at[kind, c],
            recv_sem=recv.at[to_slot, c],
            device_id=(row + step, col),
            device_id_type=pl.DeviceIdType.MESH,
        )

    def forward(slot, c, kind, step):
        return copy(out.at[slot, piece(c)], slot - step, c, kind, step)

    def arrived(slot, c):
        copy(own.at[piece(c)], slot, c, 0, sx).wait_recv()

    x_step, y_step = sx, 2 * sy
    x_slot, y_slot, d_slot = 3 + sx, 3 + 2 * sy, 3 + sx + 2 * sy
    barrier = pltpu.get_barrier_semaphore()
    for step in (x_step, y_step):
        pl.semaphore_signal(barrier, inc=1, device_id=(row + step, col), device_id_type=pl.DeviceIdType.MESH)
    for way in (-1, 1):
        @pl.when(exists(way))
        def _():
            pl.semaphore_signal(barrier, inc=1, device_id=(row + GROUP * way, col), device_id_type=pl.DeviceIdType.MESH)
    pl.semaphore_wait(barrier, 2 + exists(-1).astype(jnp.int32) + exists(1).astype(jnp.int32))

    half = CHUNKS // 2
    started = []

    def go(make, when=None):
        started.append((make, when))
        if when is None:
            make().start()
        else:
            @pl.when(when)
            def _():
                make().start()

    for c in range(CHUNKS):
        go(lambda c=c: copy(own.at[piece(c)], 3 - sx, c, 0, x_step))
        go(lambda c=c: copy(own.at[piece(c)], 3 - 2 * sy, c, 1, y_step))
    for c in range(CHUNKS):
        arrived(x_slot, c)
        if c < half:
            go(lambda c=c: forward(x_slot, c, 2, y_step))
        go(lambda c=c: forward(x_slot, c, 3, GROUP * sx), exists(sx))
        arrived(y_slot, c)
        if c >= half:
            go(lambda c=c: forward(y_slot, c, 2, x_step))
        go(lambda c=c: forward(y_slot, c, 4, GROUP * sy), exists(sy))
    a_slot, b_slot = 3 - 2 * sy, 3 - 3 * sx
    for c in range(CHUNKS):
        arrived(d_slot, c)
        go(lambda c=c: forward(d_slot, c, 5, GROUP * sy), middle & exists(sy))
        @pl.when(exists(-sy))
        def _():
            arrived(a_slot, c)
        if c < half:
            go(lambda c=c: forward(a_slot, c, 6, x_step), middle & exists(-sy))
        @pl.when(exists(-sx))
        def _():
            arrived(b_slot, c)
        if c >= half:
            go(lambda c=c: forward(b_slot, c, 6, y_step), middle & exists(-sx))
    for c in range(CHUNKS):
        @pl.when(middle & exists(-sy))
        def _():
            arrived(3 - 3 * sy, c)
        @pl.when(outer & exists(-sx))
        def _():
            arrived(3 - sx, c)
    for make, when in started:
        if when is None:
            make().wait_send()
        else:
            @pl.when(when)
            def _():
                make().wait_send()


def gather_blocks(combined, peers):
    anywhere = pl.BlockSpec(memory_space=pl.ANY)
    return pl.pallas_call(
        functools.partial(gather_kernel, peers),
        out_shape=jax.ShapeDtypeStruct((2 * NEIGHBOR + 1,) + combined.shape, combined.dtype),
        in_specs=[anywhere],
        out_specs=anywhere,
        scratch_shapes=[pltpu.SemaphoreType.DMA((2 * NEIGHBOR + 1, CHUNKS)), pltpu.SemaphoreType.DMA((7, CHUNKS))],
        compiler_params=pltpu.CompilerParams(collective_id=0, has_side_effects=True),
        name="gather",
    )(combined)


def swapped(array, axis, bit):
    return lax.ppermute(array, axis, [(i, i ^ 1 << bit) for i in range(lax.axis_size(axis))])


def turned(array, axis, by):
    peers = lax.axis_size(axis)
    return lax.ppermute(array, axis, [(i, (i + by) % peers) for i in range(peers)])


def gathered(array, axis):
    peers = lax.axis_size(axis)
    if peers == 2:
        other = turned(array, axis, 1)
        first = lax.axis_index(axis) == 0
        return jnp.concatenate([jnp.where(first, array, other), jnp.where(first, other, array)], axis=-2)
    return lax.all_gather(array, axis, axis=array.ndim - 2, tiled=True)


def sample_kernel(inv_width, slots, rows_ref, own_ref, near_ref, out_ref, buf, sems):
    entries = buf.shape[0] + 1
    width = rows_ref.shape[1]
    copies = [pltpu.make_async_copy(near_ref.at[slots[e]], buf.at[e - 1], sems.at[e - 1]) for e in range(1, entries)]
    for copy in copies:
        copy.start()
    tile = 256
    for e in range(entries):
        if e:
            copies[e - 1].wait()
        block = own_ref if e == 0 else buf.at[e - 1]

        def body(i, carry):
            at = pl.ds(pl.multiple_of(i * tile, tile), tile)
            scores = lax.dot_general(
                rows_ref[at, :], block[:, 0:width], (((1,), (1,)), ((), ())), preferred_element_type=F32
            )
            kernel = jnp.exp(scores * inv_width).astype(jnp.bfloat16)
            term = jnp.dot(kernel, block[:, width:], preferred_element_type=F32)
            out_ref[at, :] = term if e == 0 else out_ref[at, :] + term
            return carry

        lax.fori_loop(0, rows_ref.shape[0] // tile, body, 0)


def sample_sum(slots, part_rows, combined, near):
    vm = pl.BlockSpec(memory_space=pltpu.VMEM)
    sketch_width = combined.shape[1] - part_rows.shape[1]
    return pl.pallas_call(
        functools.partial(sample_kernel, 1.0 / D),
        out_shape=jax.ShapeDtypeStruct((part_rows.shape[0], sketch_width), F32),
        in_specs=[pl.BlockSpec(memory_space=pltpu.SMEM), vm, vm, pl.BlockSpec(memory_space=pl.ANY)],
        out_specs=vm,
        scratch_shapes=[pltpu.VMEM((NEAR - 1,) + combined.shape, combined.dtype), pltpu.SemaphoreType.DMA((NEAR - 1,))],
        compiler_params=pltpu.CompilerParams(vmem_limit_bytes=48 * 2**20),
        name="sample",
    )(slots, part_rows, combined, near)


def shards(features, sketch, near_blocks):
    col_count = lax.axis_size("col")
    own_count = features.shape[0]
    leaf_rows = own_count * col_count
    row_index = lax.axis_index("row")
    col_index = lax.axis_index("col")
    sample_norm = 1.0 / math.sqrt(8 * NEAR * LEAF)
    pieces = [features] + [turned(features, "col", -s) for s in range(1, col_count)]
    part_rows = jnp.concatenate(pieces, axis=0)
    combined = jnp.concatenate([features, sketch], axis=1)
    near = gather_blocks(combined, lax.axis_size("row"))
    running = sample_sum(near_blocks[0] - row_index + NEIGHBOR, part_rows, combined, near)
    own_sample = running[:own_count]
    for s in range(1, col_count):
        own_sample = own_sample + turned(running[s * own_count:(s + 1) * own_count], "col", s)
    own_sample = own_sample * sample_norm + 0.5 * sketch.astype(F32)
    gram = lax.dot_general(
        own_sample[:, :RANK], own_sample, TN, precision=GRAM_PRECISION, preferred_element_type=F32
    ) / leaf_rows
    if col_count == 2:
        gram = gram + turned(gram, "col", 1)
    else:
        gram = lax.psum(gram, "col")
    slab = RANK // col_count
    first = col_index * slab
    part = lax.dynamic_slice(gram, (first, 0), (slab, RANK))
    parts = []
    for depth_level in range(LEVELS):
        part = (part + swapped(part, "row", depth_level)) * 0.5
        parts.append(part)
    level = gathered(jnp.stack(parts), "col")
    leaf_basis, residual, factors = factor(gram, level, own_sample, first.astype(jnp.int32)[None], slab)
    return leaf_basis, residual, factors[None]


GRAM_PRECISION = lax.Precision.HIGHEST


def solution(mesh):
    return jax.shard_map(
        shards,
        mesh=mesh,
        in_specs=(P(("row", "col"), None), P(("row", "col"), None), P("row", None)),
        out_specs=(P(("row", "col"), None), P(("row", "col"), None), P("row", None, "col", None)),
        check_vma=False,
    )
```
